32 devices in a mesh: img: 8 (over z, y), ch: 4 (over x, core).
Axes of the slice: x: 2, y: 2, z: 4, core: 2. Of those that a mesh axis runs over, the one named last changes fastest.
Arguments:
- kspace_data: float32 [4, 12, 2, 320, 320], P('ch', None, None, None, 'img'), may hold values from -6 to 6
- coil_maps: float32 [4, 12, 2, 320, 320], P('ch', None, None, 'img'), may hold values from -2.3 to 2.3
- sample_mask: int32 [4, 320, 320], P('ch', None, 'img'), may hold values 0 or 1
- valid_mask: int32 [4, 320, 320], P(None, 'img'), may hold values from 0 to 1, as said below
- target: float32 [4, 2, 320, 320], P('ch', None, 'img'), may hold values from -11.3 to 11.3
- first_weight: float32 [9, 64, 2], P(None, 'ch'), may hold values from -1.5 to 1.5
- middle_weights: float32 [3, 9, 64, 64], P(None, None, 'ch'), may hold values from -0.25 to 0.25
- last_weight: float32 [9, 2, 64], P(None, None, 'ch'), may hold values from -0.25 to 0.25
- norm_params: float32 [4, 2, 64], P(None, None, 'ch'), may hold values from 0.2 to 1.5
- penalty: float32 [1], replicated, may hold values from 0.03 to 0.08
- first_mean: float32 [9, 64, 2], P(None, 'ch'), may hold values from -0.0017089844 to 0.0017089844
- first_square: float32 [9, 64, 2], P(None, 'ch'), may hold values from 1e-08 to 4e-08
- middle_mean: float32 [3, 9, 64, 64], P(None, None, 'ch'), may hold values from -0.0017089844 to 0.0017089844
- middle_square: float32 [3, 9, 64, 64], P(None, None, 'ch'), may hold values from 1e-08 to 4e-08
- last_mean: float32 [9, 2, 64], P(None, None, 'ch'), may hold values from -0.0017089844 to 0.0017089844
- last_square: float32 [9, 2, 64], P(None, None, 'ch'), may hold values from 1e-08 to 4e-08
- norm_mean: float32 [4, 2, 64], P(None, None, 'ch'), may hold values from -0.0017089844 to 0.0017089844
- norm_square: float32 [4, 2, 64], P(None, None, 'ch'), may hold values from 1e-08 to 4e-08
- penalty_mean: float32 [1], replicated, may hold values from -0.3125 to 0.3125
- penalty_square: float32 [1], replicated, may hold values from 0.00025 to 0.001
- step_count: int32 [1], replicated, may hold values from 1 to 20
Outputs:
- loss_value: float32 [], replicated
- first_new: float32 [9, 64, 2], P(None, 'ch')
- first_mean_new: float32 [9, 64, 2], P(None, 'ch')
- first_square_new: float32 [9, 64, 2], P(None, 'ch')
- middle_new: float32 [3, 9, 64, 64], P(None, None, 'ch')
- middle_mean_new: float32 [3, 9, 64, 64], P(None, None, 'ch')
- middle_square_new: float32 [3, 9, 64, 64], P(None, None, 'ch')
- last_new: float32 [9, 2, 64], P(None, None, 'ch')
- last_mean_new: float32 [9, 2, 64], P(None, None, 'ch')
- last_square_new: float32 [9, 2, 64], P(None, None, 'ch')
- norm_new: float32 [4, 2, 64], P(None, None, 'ch')
- norm_mean_new: float32 [4, 2, 64], P(None, None, 'ch')
- norm_square_new: float32 [4, 2, 64], P(None, None, 'ch')
- penalty_state: float32 [3], replicated
The draws below stay inside these ranges and needn't reach their ends.
Inputs may be any that keep to these rules, and one draw needn't show every extreme that they name: `valid_mask`: each image's ones fill one rectangle of at least 160 rows and 160 columns.
All inputs are finite; a program needn't handle non-finite values. No bound on the sum of `sample_mask` on one device may be relied on, other than what follows from the above.
Results may differ from the reference program's by a relative error of at most 0.0053.
Values may be sent and summed in bfloat16 or wider, within the bound.
No kernel may reach another device: no remote copies, remote signals or barrier semaphores. Data moves between devices by JAX's collectives and lax.ppermute only.
A program may use at most 576 MiB of HBM per device.

```python
import math
import jax
import jax.numpy as jnp
from jax import lax

NB = 4
COILS = 12
H = 320
W = 320
C = 64
UNROLLS = 1
CG_ITERS = 2


def draw_valid_mask(key, part):
    subkeys = jax.random.split(key, 4)
    row_span = jax.random.randint(subkeys[0], (NB,), H // 2, H + 1)
    col_span = jax.random.randint(subkeys[1], (NB,), W // 2, W + 1)
    row_begin = jax.random.randint(subkeys[2], (NB,), 0, H - row_span + 1)
    col_begin = jax.random.randint(subkeys[3], (NB,), 0, W - col_span + 1)
    row_index = jnp.arange(H, dtype=jnp.int32)[None, :, None]
    col_index = jnp.arange(W, dtype=jnp.int32)[None, None, :]
    inside_rows = (row_index >= row_begin[:, None, None]) & (row_index < (row_begin + row_span)[:, None, None])
    inside_cols = (col_index >= col_begin[:, None, None]) & (col_index < (col_begin + col_span)[:, None, None])
    return (inside_rows & inside_cols).astype(jnp.int32)


def row_profile(key, low_end, high_end):
    position = jnp.arange(H, dtype=jnp.float32) / float(H - 1)
    envelope = low_end * jnp.exp(position * jnp.log(high_end / low_end))
    rough = jax.random.uniform(key, (H,), jnp.float32, 0.7, 1.4)
    return envelope * rough


def draw_coil_maps(key, part):
    keys = jax.random.split(jax.random.fold_in(key, 11), 2)
    shape = (NB, COILS, 2, H, W)
    base = jnp.clip(jax.random.normal(keys[0], shape, jnp.float32), -3.0, 3.0)
    profile = row_profile(keys[1], 0.6, 1.8)
    return 0.3 * base * profile[None, None, None, :, None]


def draw_target(key, part):
    keys = jax.random.split(jax.random.fold_in(key, 23), 2)
    shape = (NB, 2, H, W)
    base = jnp.clip(jax.random.normal(keys[0], shape, jnp.float32), -4.0, 4.0)
    profile = row_profile(keys[1], 0.5, 2.0)
    return base * profile[None, None, :, None]


def plant(result, own_key, low, largest):
    spot = [jax.random.randint(jax.random.fold_in(own_key, axis), (), 0, length) for axis, length in enumerate(result.shape)]
    main_axis = result.shape.index(max(result.shape))
    next_to = spot[:main_axis] + [(spot[main_axis] + 1) % result.shape[main_axis]] + spot[main_axis + 1:]
    return result.at[tuple(spot)].set(low).at[tuple(next_to)].set(largest)


def block_scale(key, dims, pieces, least, high):
    factor_of, own = 1.0, jax.random.fold_in(key, 6)
    for axis_at, parts in pieces:
        draws = jnp.exp(jax.random.uniform(jax.random.fold_in(own, axis_at), (parts,), jnp.float32, least / len(pieces), high / len(pieces)))
        factor_of = factor_of * jnp.repeat(draws, dims[axis_at] // parts).reshape([-1 if axis == axis_at else 1 for axis in range(len(dims))])
    return factor_of


def normal_values(key, shape, spread, most, pieces=(), kind=jnp.bfloat16):
    gain = block_scale(key, shape, pieces, -0.22, 0.18) if pieces else 1.0
    result = jax.random.normal(key, shape, jnp.float32) * spread * gain
    return jnp.minimum(jnp.maximum(result, -most), most).astype(kind)


def setup_inputs(seed: int = 0) -> dict:
    splits = jax.random.split(jax.random.key(seed), 22)
    return {
        "kspace_data": normal_values(splits[0], (NB, COILS, 2, H, W), 1.0, 6.0, ((0, 4), (4, 8)), jnp.float32),
        "coil_maps": draw_coil_maps(jax.random.fold_in(splits[21], 71), 0),
        "sample_mask": plant((jax.random.randint(splits[2], (NB, H, W), 0, 3) < 1).astype(jnp.int32), jax.random.fold_in(splits[2], 1), 0, 1),
        "valid_mask": draw_valid_mask(jax.random.fold_in(splits[21], 71), 0),
        "target": draw_target(jax.random.fold_in(splits[21], 71), 0),
        "first_weight": normal_values(splits[5], (9, C, 2), 18 ** -0.5, 1.5, ((1, 4),), jnp.float32),
        "middle_weights": normal_values(splits[6], (3, 9, C, C), (9 * C) ** -0.5, 0.25, ((2, 4),), jnp.float32),
        "last_weight": normal_values(splits[7], (9, 2, C), (9 * C) ** -0.5, 0.25, ((2, 4),), jnp.float32),
        "norm_params": jnp.clip(0.2 + 1.3 * jax.random.uniform(splits[8], (4, 2, C), jnp.float32) ** block_scale(splits[8], (4, 2, C), ((2, 4),), -0.2, 0.2), 0.2, 1.5),
        "penalty": jnp.clip(jax.random.uniform(splits[9], (1,), jnp.float32, 0.03, 0.08), 0.03, 0.08),
        "first_mean": normal_values(splits[10], (9, C, 2), 0.0003, 0.0017089844, ((1, 4),), jnp.float32),
        "first_square": jnp.clip(jnp.exp(math.log(3.999999975690116e-08) - 1.3862944 * jax.random.uniform(splits[11], (9, C, 2), jnp.float32) ** block_scale(splits[11], (9, C, 2), ((1, 4),), -0.2, 0.2)), 9.99999993922529e-09, 3.999999975690116e-08),
        "middle_mean": normal_values(splits[12], (3, 9, C, C), 0.0003, 0.0017089844, ((2, 4),), jnp.float32),
        "middle_square": jnp.clip(jnp.exp(math.log(3.999999975690116e-08) - 1.3862944 * jax.random.uniform(splits[13], (3, 9, C, C), jnp.float32) ** block_scale(splits[13], (3, 9, C, C), ((2, 4),), -0.2, 0.2)), 9.99999993922529e-09, 3.999999975690116e-08),
        "last_mean": normal_values(splits[14], (9, 2, C), 0.0003, 0.0017089844, ((2, 4),), jnp.float32),
        "last_square": jnp.clip(jnp.exp(math.log(3.999999975690116e-08) - 1.3862944 * jax.random.uniform(splits[15], (9, 2, C), jnp.float32) ** block_scale(splits[15], (9, 2, C), ((2, 4),), -0.2, 0.2)), 9.99999993922529e-09, 3.999999975690116e-08),
        "norm_mean": normal_values(splits[16], (4, 2, C), 0.0003, 0.0017089844, ((2, 4),), jnp.float32),
        "norm_square": jnp.clip(jnp.exp(math.log(3.999999975690116e-08) - 1.3862944 * jax.random.uniform(splits[17], (4, 2, C), jnp.float32) ** block_scale(splits[17], (4, 2, C), ((2, 4),), -0.2, 0.2)), 9.99999993922529e-09, 3.999999975690116e-08),
        "penalty_mean": normal_values(splits[18], (1,), 0.05, 0.3125, (), jnp.float32),
        "penalty_square": jnp.clip(jnp.exp(jax.random.uniform(splits[19], (1,), jnp.float32, math.log(0.00025), math.log(0.001))), 0.00025, 0.001),
        "step_count": jax.random.randint(splits[20], (1,), 1, 21).astype(jnp.int32),
    }


highest = lax.Precision.HIGHEST
norm_epsilon = 1e-05
beta_one = 0.9
beta_two = 0.999
adam_epsilon = 1e-08
decay_rate = 0.01
rate_conv = 0.04
rate_norm = 0.1
rate_penalty = 0.01

@jax.custom_vjp
def low(v):
    return lax.optimization_barrier(v.astype(jnp.bfloat16)).astype(jnp.float32)

@jax.custom_vjp
def low_back(v):
    return v

def low_keep(v):
    return (low(v), None)

def low_pass(kept, grad):
    return (grad,)

def back_keep(v):
    return (v, None)

def back_low(kept, grad):
    return (low(grad),)
low.defvjp(low_keep, low_pass)
low_back.defvjp(back_keep, back_low)

def planes_of(field):
    return jnp.stack([field.real, field.imag], axis=1)

def adjoint_data(kspace_data, coil_field, sample_field):
    measured = (kspace_data[:, :, 0] + 1j * kspace_data[:, :, 1]) * sample_field[:, None]
    coil_images = jnp.fft.ifft2(measured, norm='ortho')
    return planes_of(lax.optimization_barrier(jnp.sum(jnp.conj(coil_field) * coil_images, axis=1)))

def normal_apply(search, coil_field, sample_field, penalty_value):
    complex_search = search[:, 0] + 1j * search[:, 1]
    spectra = jnp.fft.fft2(coil_field * complex_search[:, None], norm='ortho') * sample_field[:, None]
    combined = lax.optimization_barrier(jnp.sum(jnp.conj(coil_field) * jnp.fft.ifft2(spectra, norm='ortho'), axis=1))
    return planes_of(combined) + penalty_value * search

def inner(left, right):
    return lax.optimization_barrier(jnp.sum(left * right, axis=(1, 2, 3)))[:, None, None, None]

def solve(right_side, coil_field, sample_field, penalty_value):
    iterate = jnp.zeros_like(right_side)
    residual = right_side
    search = right_side
    norm_now = inner(residual, residual)
    for sweep in range(CG_ITERS):
        image = normal_apply(search, coil_field, sample_field, penalty_value)
        alpha = norm_now / inner(search, image)
        iterate = iterate + alpha * search
        residual = residual - alpha * image
        norm_next = inner(residual, residual)
        search = residual + norm_next / norm_now * search
        norm_now = norm_next
    return iterate

def conv_layer(activation, weight):
    kernel = weight.reshape(3, 3, weight.shape[1], weight.shape[2]).transpose(2, 3, 0, 1)
    return lax.conv_general_dilated(activation, kernel, (1, 1), ((1, 1), (1, 1)), dimension_numbers=('NCHW', 'OIHW', 'NCHW'), precision=highest)

def norm_relu(hidden, gain_bias, valid_field, pixel_count):
    weight_mask = valid_field[:, None]
    average = lax.optimization_barrier(jnp.sum(weight_mask * hidden, axis=(0, 2, 3))) / pixel_count
    second = lax.optimization_barrier(jnp.sum(weight_mask * hidden * hidden, axis=(0, 2, 3))) / pixel_count
    scale_inv = lax.rsqrt(second - average * average + norm_epsilon)
    normed = (hidden - average[None, :, None, None]) * scale_inv[None, :, None, None]
    shaped = gain_bias[0][None, :, None, None] * normed + gain_bias[1][None, :, None, None]
    return jnp.maximum(shaped, 0.0)

def denoise(field, first_low, middle_low, last_low, norm_params, valid_field, pixel_count):
    activation = low(field)
    hidden = low_back(conv_layer(activation, first_low))
    activation = low(norm_relu(hidden, norm_params[0], valid_field, pixel_count))
    for layer in range(3):
        hidden = low_back(conv_layer(activation, middle_low[layer]))
        activation = low(norm_relu(hidden, norm_params[layer + 1], valid_field, pixel_count))
    return field + low_back(conv_layer(activation, last_low))

def adamw(weight, grad, first_m, second_m, rate, decay, step_value):
    mean_new = beta_one * first_m + (1.0 - beta_one) * grad
    square_new = beta_two * second_m + (1.0 - beta_two) * grad * grad
    mean_hat = mean_new / (1.0 - beta_one ** step_value)
    square_hat = square_new / (1.0 - beta_two ** step_value)
    updated = weight - rate * (mean_hat / (jnp.sqrt(square_hat) + adam_epsilon) + decay * weight)
    return (updated, mean_new, square_new)

def reference(kspace_data, coil_maps, sample_mask, valid_mask, target, first_weight, middle_weights, last_weight, norm_params, penalty, first_mean, first_square, middle_mean, middle_square, last_mean, last_square, norm_mean, norm_square, penalty_mean, penalty_square, step_count):
    coil_field = coil_maps[:, :, 0] + 1j * coil_maps[:, :, 1]
    sample_field = sample_mask.astype(jnp.float32)
    valid_field = valid_mask.astype(jnp.float32)
    pixel_count = jnp.sum(valid_field)
    initial = adjoint_data(kspace_data, coil_field, sample_field)
    smoothed = jax.checkpoint(denoise)

    def objective(first_w, middle_w, last_w, norms, penalty_w):
        first_low = low(first_w)
        middle_low = low(middle_w)
        last_low = low(last_w)
        field = initial
        for unroll in range(UNROLLS):
            denoised = smoothed(field, first_low, middle_low, last_low, norms, valid_field, pixel_count)
            field = solve(initial + penalty_w[0] * denoised, coil_field, sample_field, penalty_w[0])
        difference = field - target
        return jnp.sum(valid_field[:, None] * difference * difference) / pixel_count
    loss_value, pullback = jax.vjp(objective, first_weight, middle_weights, last_weight, norm_params, penalty)
    grad_first, grad_middle, grad_last, grad_norms, grad_penalty = pullback(jnp.ones_like(loss_value))
    step_value = step_count[0].astype(jnp.float32) + 1.0
    first_new, first_mean_new, first_square_new = adamw(first_weight, grad_first, first_mean, first_square, rate_conv, decay_rate, step_value)
    middle_new, middle_mean_new, middle_square_new = adamw(middle_weights, grad_middle, middle_mean, middle_square, rate_conv, decay_rate, step_value)
    last_new, last_mean_new, last_square_new = adamw(last_weight, grad_last, last_mean, last_square, rate_conv, decay_rate, step_value)
    norm_new, norm_mean_new, norm_square_new = adamw(norm_params, grad_norms, norm_mean, norm_square, rate_norm, 0.0, step_value)
    penalty_new, penalty_mean_new, penalty_square_new = adamw(penalty, grad_penalty, penalty_mean, penalty_square, rate_penalty, 0.0, step_value)
    penalty_state = jnp.concatenate([penalty_new, penalty_mean_new, penalty_square_new])
    return (loss_value, first_new, first_mean_new, first_square_new, middle_new, middle_mean_new, middle_square_new, last_new, last_mean_new, last_square_new, norm_new, norm_mean_new, norm_square_new, penalty_state)
```

```python
import math

import jax
import jax.numpy as jnp
import numpy as np
from jax import lax
from jax.experimental import pallas as pl
from jax.experimental.pallas import tpu as pltpu
from jax.sharding import PartitionSpec as P

norm_epsilon = 1e-05
beta_one = 0.9
beta_two = 0.999
adam_epsilon = 1e-08
decay_rate = 0.01
rate_conv = 0.04
rate_norm = 0.1
rate_penalty = 0.01

BOTH = ("img", "ch")
f32 = jnp.float32
bf16 = jnp.bfloat16
CH = 64
LANES = 384
HALO = 7


def rup(n, m):
    return (n + m - 1) // m * m


def params():
    return pltpu.CompilerParams(vmem_limit_bytes=60 * 1024 * 1024)


def call(kernel, outs, *args, scratch=(), name=None):
    return pl.pallas_call(
        kernel,
        out_shape=[jax.ShapeDtypeStruct(s, d) for s, d in outs],
        scratch_shapes=list(scratch),
        compiler_params=params(),
        name=name,
    )(*args)


def dft_tables(n):
    k = np.arange(n)
    angle = (k[:, None] * k[None, :] % n) * (2.0 * math.pi / n)
    cosine = np.cos(angle) / math.sqrt(n)
    sine = np.sin(angle) / math.sqrt(n)
    right_forward = np.block([[cosine, -sine], [sine, cosine]])
    right_back = np.block([[cosine, sine], [-sine, cosine]])
    left = np.concatenate([cosine, sine], 0)
    return tuple(jnp.asarray(t.astype(np.float32)).astype(bf16) for t in (right_forward, right_back, left))


def swap(values):
    return pltpu.roll(values, values.shape[-1] // 2, values.ndim - 1)


def first_half(shape):
    return lax.broadcasted_iota(jnp.int32, shape, len(shape) - 1) < shape[-1] // 2


def mm(a, b):
    return jnp.dot(a, b, preferred_element_type=f32)


def left_dft(left, values, inverse):
    rows = left.shape[0] // 2
    both = mm(left, values)
    plain, crossed = both[:rows], swap(both[rows:])
    half = first_half(plain.shape)
    crossed = jnp.where(half, crossed, -crossed)
    return plain - crossed if inverse else plain + crossed


def map_pair(cat):
    half = first_half(cat.shape)
    other = swap(cat)
    return jnp.where(half, cat, other), jnp.where(half, -other, cat)


def spec_rows_kernel(kspace, mask, left, out, gathered):
    coils, _, _, cols = kspace.shape
    wide = gathered.shape[1] // 2
    gathered[...] = jnp.zeros(gathered.shape, f32)
    m = mask[...].astype(f32)
    for part in range(2):
        for coil in range(coils):
            gathered[:, part * wide + coil * cols : part * wide + (coil + 1) * cols] = kspace[coil, part] * m
    out[...] = left_dft(left[...], gathered[...].astype(bf16), True).astype(bf16)


def initial_kernel(spec, maps, right_back, out, gathered, cat):
    sources, rows, wide2 = spec.shape
    coils = maps.shape[0]
    wide = wide2 // 2
    width = maps.shape[3]
    cols = width // sources
    stride = gathered.shape[0] // coils
    if stride > rows:
        gathered[...] = jnp.zeros(gathered.shape, f32)
    for s in range(sources):
        block = spec[s].astype(f32)
        for part in range(2):
            for coil in range(coils):
                at = part * wide + coil * cols
                to = part * width + s * cols
                gathered[coil * stride : coil * stride + rows, to : to + cols] = block[:, at : at + cols]
    full = mm(gathered[...].astype(bf16), right_back[...])
    total = jnp.zeros((rows, 2 * width), f32)
    for coil in range(coils):
        cat[:, :width] = maps[coil, 0]
        cat[:, width:] = maps[coil, 1]
        real, imag = map_pair(cat[...])
        values = full[coil * stride : coil * stride + rows]
        total = total + real * values - imag * swap(values)
    out[...] = total


def apply_coils(vector, maps, mask2, right_forward, right_back, left):
    total = jnp.zeros(vector.shape, f32)
    other = swap(vector)
    for coil in range(maps.shape[0]):
        real, imag = map_pair(maps[coil].astype(f32))
        sent = (real * vector + imag * other).astype(bf16)
        step = mm(sent, right_forward[...]).astype(bf16)
        step = left_dft(left[...], step, False) * mask2
        step = left_dft(left[...], step.astype(bf16), True).astype(bf16)
        step = mm(step, right_back[...])
        total = total + real * step - imag * swap(step)
    return total


def dot_all(a, b):
    return jnp.sum(a * b)


def solve_first_kernel(right, maps, mask2, right_forward, right_back, left, out):
    vector = right[...].astype(f32)
    out[...] = apply_coils(vector, maps, mask2[...], right_forward, right_back, left).astype(bf16)


def first_step(right, applied, penalty):
    b = right.astype(f32)
    q0 = applied.astype(f32) + penalty * b
    rr0 = dot_all(b, b)
    pq0 = dot_all(b, q0)
    alpha0 = rr0 / pq0
    r1 = b - alpha0 * q0
    rn0 = dot_all(r1, r1)
    ratio0 = rn0 / rr0
    p1 = r1 + ratio0 * b
    return b, q0, rr0, pq0, alpha0, r1, rn0, ratio0, p1


def solve_second_kernel(right, applied0, maps, mask2, penalty, right_forward, right_back, left, out):
    p1 = first_step(right[...], applied0[...], penalty[0])[-1]
    out[...] = apply_coils(p1, maps, mask2[...], right_forward, right_back, left).astype(bf16)


def solve_back_kernel(
    right, applied0, applied1, maps, mask2, target, valid2, penalty, count,
    right_forward, right_back, left, out, rest, scalars
):
    lam = penalty[0]
    b, q0, rr0, pq0, alpha0, r1, rn0, ratio0, p1 = first_step(
        right[...], applied0[...], lam
    )
    q1 = applied1[...].astype(f32) + lam * p1
    pq1 = dot_all(p1, q1)
    alpha1 = rn0 / pq1
    x = alpha0 * b + alpha1 * p1
    difference = valid2[...] * (x - target[...])
    loss = dot_all(difference, difference) / count[0]
    gx = difference * (2.0 / count[0])
    ga1 = dot_all(gx, p1)
    gpq1 = -ga1 * alpha1 / pq1
    gp = alpha1 * gx + (2.0 * gpq1) * q1
    pen = gpq1 * dot_all(p1, p1)
    grr1 = ga1 / pq1
    d1 = dot_all(gp, b)
    d2 = dot_all(gx, b)
    d4 = dot_all(gp, q0)
    d5 = dot_all(r1, q0)
    grn = grr1 + d1 / rr0
    ga = d2 - d4 - 2.0 * grn * d5
    gr = gp + (2.0 * grn) * r1
    gpq = -ga * alpha0 / pq0
    gq = gpq * b - alpha0 * gr
    grr = ga / pq0 - d1 * rn0 / (rr0 * rr0)
    pen = pen + dot_all(gq, b)
    rest[...] = gr + ratio0 * gp + alpha0 * gx + gpq * q0 + (2.0 * grr) * b + lam * gq
    out[...] = apply_coils(gq, maps, mask2[...], right_forward, right_back, left).astype(bf16)
    lane = lax.broadcasted_iota(jnp.int32, scalars.shape, 1)
    scalars[...] = jnp.where(lane == 0, loss, jnp.where(lane == 1, pen, 0.0))


def per_channel(row):
    turned = jnp.transpose(jnp.broadcast_to(row, (128, 128)))
    tiled = jnp.concatenate([turned] * (LANES // 128), axis=1)
    return tiled[:CH], tiled[CH:]


def gathered_sums(stats):
    values = stats[...]
    row = lax.broadcasted_iota(jnp.int32, values.shape, 0) % 2
    sums = jnp.sum(jnp.where(row == 0, values, 0.0), axis=0, keepdims=True)
    counts = jnp.sum(jnp.where(row == 1, values, 0.0), axis=0, keepdims=True)
    return sums, counts[:, :1]


def norm_terms(stats, gain_bias):
    sums, count = gathered_sums(stats)
    means = sums / count
    average, second = per_channel(means)
    rstd = lax.rsqrt(second - average * average + norm_epsilon)
    gain, bias = per_channel(gain_bias[...])
    return average, rstd, gain, bias


def fold(values):
    return sum(values[:, 128 * t : 128 * (t + 1)] for t in range(LANES // 128))


def loop(count, step, carry):
    unroll = 2 if count % 2 == 0 else 1

    def several(t, state):
        for u in range(unroll):
            state = step(t * unroll + u, state)
        return state

    return lax.fori_loop(0, count // unroll, several, carry)


def write_sums(out, acc1, acc2, extra):
    both = jnp.concatenate([acc1, acc2], axis=0)
    row = jnp.sum(jnp.transpose(both), axis=0, keepdims=True)
    second = jnp.broadcast_to(extra, row.shape)
    which = lax.broadcasted_iota(jnp.int32, out.shape, 0) % 2
    out[...] = jnp.where(which == 0, row, second)


def conv_row(weight, stacked):
    y = mm(weight, stacked)
    n = y.shape[0] // 3
    return pltpu.roll(y[:n], 1, 1) + y[n : 2 * n] + pltpu.roll(y[2 * n :], LANES - 1, 1)


def first_conv_kernel(stacked, weight, mask, count, hidden, sums):
    w = weight[...]

    def row(r, acc):
        out = conv_row(w, stacked[r])
        hidden[r] = out
        kept = out * mask[pl.ds(r, 1), :]
        return acc[0] + fold(kept), acc[1] + fold(kept * out)

    zero = jnp.zeros((CH, 128), f32)
    acc = loop(hidden.shape[0], row, (zero, zero))
    write_sums(sums, *acc, count[0])


def conv_kernel(hidden, stats, gain_bias, weight, inside, mask, count, act, out, sums):
    average, rstd, gain, bias = norm_terms(stats, gain_bias)
    scale = gain * rstd
    shift = bias - average * scale
    w = weight[...]

    def activate(r):
        act[r] = (jnp.maximum(hidden[r] * scale + shift, 0.0) * inside[pl.ds(r, 1), :]).astype(bf16)

    activate(0)
    activate(1)

    def row(r, acc):
        activate(r + 2)
        value = conv_row(w, act[pl.ds(r, 3)].reshape(3 * CH, LANES))
        out[r] = value
        kept = value * mask[pl.ds(r, 1), :]
        return acc[0] + fold(kept), acc[1] + fold(kept * value)

    zero = jnp.zeros((CH, 128), f32)
    acc = loop(out.shape[0], row, (zero, zero))
    write_sums(sums, *acc, count[0])


def last_conv_kernel(hidden, stats, gain_bias, weight, inside, act, out, *, skip):
    average, rstd, gain, bias = norm_terms(stats, gain_bias)
    scale = gain * rstd
    shift = bias - average * scale
    w = weight[...]

    def activate(r):
        act[r] = (jnp.maximum(hidden[r + skip] * scale + shift, 0.0) * inside[pl.ds(r + skip, 1), :]).astype(bf16)

    activate(0)
    activate(1)

    def row(r, carry):
        activate(r + 2)
        out[r] = conv_row(w, act[pl.ds(r, 3)].reshape(3 * CH, LANES))
        return carry

    loop(out.shape[0], row, 0)


def grad_tail(ga, hidden_row, terms, inside_row):
    average, rstd, gain, bias = terms
    normed = (hidden_row - average) * rstd
    keep = (gain * normed + bias > 0.0) & (inside_row > 0.0)
    return jnp.where(keep, ga, 0.0), normed


def back_last_kernel(stacked, weight, hidden, stats, gain_bias, inside, own, gy, sums):
    terms = norm_terms(stats, gain_bias)
    w = weight[...]

    def row(r, acc):
        value, normed = grad_tail(conv_row(w, stacked[r]), hidden[r], terms, inside[pl.ds(r, 1), :])
        gy[r] = value
        kept = value * own[pl.ds(r, 1), :]
        return acc[0] + fold(kept), acc[1] + fold(kept * normed)

    zero = jnp.zeros((CH, 128), f32)
    acc = loop(gy.shape[0], row, (zero, zero))
    write_sums(sums, *acc, 0.0)


def hidden_grad_terms(stats, back_stats, gain_bias):
    average, rstd, gain, _ = norm_terms(stats, gain_bias)
    _, count = gathered_sums(stats)
    back, _ = gathered_sums(back_stats)
    s1, s2 = per_channel(back / count)
    return average, rstd, gain * rstd, s1, s2


def back_kernel(
    gy_in, hidden_in, stats_in, back_stats, gain_bias_in, mask,
    weight, hidden, stats, gain_bias, inside, own, grad, gy, sums, *, skip_in, skip
):
    average, rstd, scale, s1, s2 = hidden_grad_terms(stats_in, back_stats, gain_bias_in)
    terms = norm_terms(stats, gain_bias)
    w = weight[...]

    def hidden_grad(r):
        normed = (hidden_in[r + skip_in] - average) * rstd
        grad[r] = (scale * (gy_in[r] - mask[pl.ds(r, 1), :] * (s1 + normed * s2))).astype(bf16)

    hidden_grad(0)
    hidden_grad(1)

    def row(r, acc):
        hidden_grad(r + 2)
        ga = conv_row(w, grad[pl.ds(r, 3)].reshape(3 * CH, LANES))
        value, normed = grad_tail(ga, hidden[r + skip], terms, inside[pl.ds(r + skip, 1), :])
        gy[r] = value
        kept = value * own[pl.ds(r, 1), :]
        return acc[0] + fold(kept), acc[1] + fold(kept * normed)

    zero = jnp.zeros((CH, 128), f32)
    acc = loop(gy.shape[0], row, (zero, zero))
    write_sums(sums, *acc, 0.0)


def shifted(row):
    wide = row.astype(f32)
    return jnp.concatenate(
        [pltpu.roll(wide, LANES - 1, 1).astype(bf16), row.astype(bf16), pltpu.roll(wide, 1, 1).astype(bf16)], axis=0
    )


def outer(a, b):
    return lax.dot_general(a, b, (((1,), (1,)), ((), ())), preferred_element_type=f32)


def weight_grad_kernel(grad, act, out, *, rows, grad_skip, act_skip, stacked):
    step = 2 if rows % 2 == 0 else 1

    def block(t, carry):
        left = []
        right = []
        for u in range(step):
            r = t * step + u
            left.append(shifted(grad[r + grad_skip]))
            if stacked:
                right.append(act[r + act_skip])
            else:
                right.append(act[pl.ds(r + act_skip, 3)].reshape(-1, LANES))
        out[...] += outer(jnp.concatenate(left, axis=1), jnp.concatenate(right, axis=1))
        return carry

    out[...] = jnp.zeros(out.shape, f32)
    lax.fori_loop(0, rows // step, block, 0)


def first_back_kernel(gy_in, hidden_in, stats_in, back_stats, gain_bias_in, mask, stacked, out, *, hidden_skip, stack_skip):
    average, rstd, scale, s1, s2 = hidden_grad_terms(stats_in, back_stats, gain_bias_in)

    def row(r, carry):
        normed = (hidden_in[r + hidden_skip] - average) * rstd
        grad = scale * (gy_in[r] - mask[pl.ds(r, 1), :] * (s1 + normed * s2))
        out[...] += outer(shifted(grad), stacked[r + stack_skip])
        return carry

    out[...] = jnp.zeros(out.shape, f32)
    loop(gy_in.shape[0], row, 0)


def spread(values, axes, size):
    wide = jnp.broadcast_to(values[None], (size,) + values.shape).reshape((size * values.shape[0],) + values.shape[1:])
    return lax.all_to_all(wide, axes, 0, 0, tiled=True)


def row_shift(values, hops):
    size = lax.axis_size("img")
    pairs = [(i, i + hops) for i in range(size) if 0 <= i + hops < size]
    return lax.ppermute(values, "img", pairs)


def with_halo(values, width):
    rows = values.shape[0]
    before, after = [], []
    need, hop = width, 1
    while need > 0:
        part = min(need, rows)
        before.insert(0, row_shift(values[rows - part :], hop))
        after.append(row_shift(values[:part], -hop))
        need -= part
        hop += 1
    return jnp.concatenate(before + [values] + after, axis=0)


def planes_stack(field, width):
    rows = field.shape[0] - 2
    planes = jnp.pad(field.reshape(field.shape[0], 2, width), ((0, 0), (0, 0), (0, LANES - width)))
    stacked = jnp.concatenate([planes[i : i + rows] for i in range(3)], axis=1)
    return jnp.pad(stacked, ((0, 0), (0, 2), (0, 0))).astype(bf16)


def adamw(weight, grad, first_m, second_m, rate, decay, step_value):
    mean_new = beta_one * first_m + (1.0 - beta_one) * grad
    square_new = beta_two * second_m + (1.0 - beta_two) * grad * grad
    mean_hat = mean_new / (1.0 - beta_one**step_value)
    square_hat = square_new / (1.0 - beta_two**step_value)
    updated = weight - rate * (mean_hat / (jnp.sqrt(square_hat) + adam_epsilon) + decay * weight)
    return (updated, mean_new, square_new)


def body(
    kspace_data, coil_maps, sample_mask, valid_mask, target,
    first_weight, middle_weights, last_weight, norm_params, penalty,
    first_mean, first_square, middle_mean, middle_square, last_mean, last_square,
    norm_mean, norm_square, penalty_mean, penalty_square, step_count,
):
    n_img = lax.axis_size("img")
    n_ch = lax.axis_size("ch")
    n_all = n_img * n_ch
    own_ch = lax.axis_index("ch")
    own_img = lax.axis_index("img")
    coils = kspace_data.shape[1]
    height = kspace_data.shape[3]
    width = coil_maps.shape[4]
    rows = coil_maps.shape[3]
    cols = kspace_data.shape[4]
    wide = 2 * width
    per_dev = -(-coils // n_img)
    right_forward, right_back, left = dft_tables(width)

    lanes = rup(coils * cols, 128)
    (spec,) = call(
        spec_rows_kernel, [((height, 2 * lanes), bf16)], kspace_data[0], sample_mask[0], left,
        scratch=[pltpu.VMEM((height, 2 * lanes), f32)], name="spec_rows",
    )
    spec = lax.all_to_all(spec.reshape(n_img, rows, 2 * lanes), "img", 0, 0, tiled=True)
    (initial,) = call(
        initial_kernel, [((rows, wide), f32)], spec, coil_maps[0], right_back,
        scratch=[pltpu.VMEM((coils * rup(rows, 8), wide), f32), pltpu.VMEM((rows, wide), f32)], name="initial",
    )

    packed = jnp.concatenate(
        [middle_weights.reshape(-1), first_weight.reshape(-1), last_weight.reshape(-1), norm_params.reshape(-1)]
    )
    packed = jnp.pad(packed, (0, rup(packed.size, 1024) - packed.size)).reshape(-1, 128)
    everyone = spread(packed, "ch", n_ch).reshape(n_ch, -1)
    sizes = [middle_weights.size, first_weight.size, last_weight.size, norm_params.size]
    cuts = np.cumsum([0] + sizes)
    shapes = [middle_weights.shape, first_weight.shape, last_weight.shape, norm_params.shape]
    channel_dim = [2, 1, 2, 2]

    def full(k):
        piece = everyone[:, cuts[k] : cuts[k + 1]].reshape((n_ch,) + shapes[k])
        piece = jnp.moveaxis(piece, 0, channel_dim[k])
        dims = list(shapes[k])
        dims[channel_dim[k]] *= n_ch
        return piece.reshape(dims)

    middle_all, first_all, last_all, norms_all = (full(k) for k in range(4))
    low = middle_all.astype(bf16).reshape(3, 3, 3, CH, CH)
    forward_w = low.transpose(0, 2, 3, 1, 4).reshape(3, 3 * CH, 3 * CH)
    back_w = low[:, ::-1, ::-1].transpose(0, 2, 4, 1, 3).reshape(3, 3 * CH, 3 * CH)
    first_low = first_all.astype(bf16).reshape(3, 3, CH, 2)
    first_w = jnp.pad(first_low.transpose(1, 2, 0, 3).reshape(3 * CH, 6), ((0, 0), (0, 2)))
    last_low = last_all.astype(bf16).reshape(3, 3, 2, CH)
    last_w = jnp.pad(last_low.transpose(1, 2, 0, 3), ((0, 0), (0, 6), (0, 0), (0, 0))).reshape(24, 3 * CH)
    last_back_w = jnp.pad(last_low[::-1, ::-1].transpose(1, 3, 0, 2).reshape(3 * CH, 6), ((0, 0), (0, 2)))
    gain_bias = norms_all.reshape(4, 1, 2 * CH)

    maps_cat = jnp.concatenate([coil_maps[0, :, 0], coil_maps[0, :, 1]], axis=-1).astype(bf16)
    maps_cat = jnp.pad(maps_cat, ((0, per_dev * n_img - coils), (0, 0), (0, 0))).reshape(n_img, per_dev * rows, wide)
    target_cat = jnp.concatenate([target[0, 0], target[0, 1]], axis=-1).astype(bf16)
    valid_own = lax.dynamic_index_in_dim(valid_mask, own_ch, 0, keepdims=False)
    flags = jnp.concatenate([valid_own, sample_mask[0].T], axis=-1).astype(bf16)
    common = jnp.broadcast_to(jnp.concatenate([target_cat, flags], axis=0)[None], (n_img, 2 * rows, wide))
    early = lax.all_to_all(jnp.concatenate([maps_cat, common], axis=1), "img", 0, 0, tiled=True)
    early = early.reshape(n_img, per_dev + 2, rows, wide)
    maps_full = early[:, :per_dev].transpose(1, 0, 2, 3).reshape(per_dev, height, wide)
    target_full = early[:, per_dev].reshape(height, wide).astype(f32)
    flags = early[:, per_dev + 1].reshape(height, wide).astype(f32)
    valid2 = jnp.concatenate([flags[:, :width]] * 2, axis=1)
    mask2 = jnp.concatenate([flags[:, width:].T] * 2, axis=1)

    row_at = own_img * rows - HALO + jnp.arange(rows + 2 * HALO)
    in_image = ((row_at >= 0) & (row_at < height)).astype(f32)
    in_lane = (jnp.arange(LANES) < width).astype(f32)
    inside = in_image[:, None] * in_lane[None, :]
    is_own = ((row_at >= own_img * rows) & (row_at < (own_img + 1) * rows)).astype(f32)
    valid_pad = jnp.pad(valid_own.astype(bf16), ((0, 0), (0, LANES - width)))
    valid_rows = with_halo(valid_pad, 3).astype(f32)
    valid_rows = jnp.pad(valid_rows, ((HALO - 3, HALO - 3), (0, 0)))
    own_valid = valid_rows * is_own[:, None]
    own_lane = is_own[:, None] * in_lane[None, :]
    local_count = jnp.sum(valid_own.astype(f32))[None]
    vm = pl.BlockSpec(memory_space=pltpu.VMEM)
    sm = pl.BlockSpec(memory_space=pltpu.SMEM)

    def part(values, width_):
        return values[HALO - width_ : HALO + rows + width_]

    def exchange(values):
        return lax.all_to_all(values, BOTH, 0, 0, tiled=True)

    sums_shape = ((2 * n_all, 128), f32)

    stacked = planes_stack(with_halo(initial, HALO), width)
    hidden1, sums = pl.pallas_call(
        first_conv_kernel,
        out_shape=[jax.ShapeDtypeStruct((rows + 12, CH, LANES), f32), jax.ShapeDtypeStruct(*sums_shape)],
        in_specs=[vm, vm, vm, sm],
        compiler_params=params(), name="conv1",
    )(stacked, first_w, part(own_valid, 6), local_count)
    stats = [exchange(sums)]
    hidden = [hidden1]
    acts = []
    for layer in range(3):
        reach = 6 - layer
        act, out, sums = pl.pallas_call(
            conv_kernel,
            out_shape=[
                jax.ShapeDtypeStruct((rows + 2 * reach, CH, LANES), bf16),
                jax.ShapeDtypeStruct((rows + 2 * reach - 2, CH, LANES), f32),
                jax.ShapeDtypeStruct(*sums_shape),
            ],
            in_specs=[vm] * 6 + [sm], compiler_params=params(), name=f"conv{layer + 2}",
        )(
            hidden[layer], stats[layer], gain_bias[layer], forward_w[layer],
            part(inside, reach), part(own_valid, reach - 1), local_count,
        )
        acts.append(act)
        hidden.append(out)
        stats.append(exchange(sums))
    act4, branch = call(
        lambda *refs: last_conv_kernel(*refs, skip=2),
        [((rows + 2, CH, LANES), bf16), ((rows, 8, LANES), f32)],
        hidden[3], stats[3], gain_bias[3], last_w, part(inside, 3), name="conv5",
    )
    denoised = initial + branch[:, :2, :width].reshape(rows, wide)
    penalty_value = penalty[0]
    right_own = (initial + penalty_value * denoised).astype(bf16)

    right = spread(right_own, "img", n_img)
    tables = (right_forward, right_back, left)

    def reduced(partial):
        got = lax.all_to_all(partial, "img", 0, 0, tiled=True)
        return jnp.sum(got.reshape(n_img, rows, wide).astype(f32), axis=0).astype(bf16)

    (partial,) = call(
        solve_first_kernel, [((height, wide), bf16)],
        right, maps_full, mask2, *tables, name="solve1",
    )
    applied0 = spread(reduced(partial), "img", n_img)
    (partial,) = pl.pallas_call(
        solve_second_kernel,
        out_shape=[jax.ShapeDtypeStruct((height, wide), bf16)],
        in_specs=[vm, vm, vm, vm, sm, vm, vm, vm], compiler_params=params(), name="solve2",
    )(right, applied0, maps_full, mask2, penalty, *tables)
    applied1 = spread(reduced(partial), "img", n_img)
    count = jnp.sum(stats[0][1::2, 0])[None]
    partial, rest, scalars = pl.pallas_call(
        solve_back_kernel,
        out_shape=[
            jax.ShapeDtypeStruct((height, wide), bf16),
            jax.ShapeDtypeStruct((height, wide), f32),
            jax.ShapeDtypeStruct((8, 128), f32),
        ],
        in_specs=[vm] * 7 + [sm, sm] + [vm] * 3, compiler_params=params(), name="solve3",
    )(right, applied0, applied1, maps_full, mask2, target_full, valid2, penalty, count, *tables)
    reach = 4
    tall = jnp.pad(partial, ((reach, reach), (0, 0)))
    windows = jnp.concatenate([tall[rows * d : rows * d + rows + 2 * reach] for d in range(n_img)], axis=0)
    windows = lax.all_to_all(windows, "img", 0, 0, tiled=True).reshape(n_img, rows + 2 * reach, wide)
    rest_own = lax.dynamic_slice_in_dim(jnp.pad(rest, ((reach, reach), (0, 0))), own_img * rows, rows + 2 * reach, 0)
    grad_right = rest_own + jnp.sum(windows.astype(f32), axis=0)
    pen_part = scalars[0, 1] / n_img + jnp.sum(grad_right[reach : reach + rows] * denoised)
    loss_part = scalars[0, 0] / n_img
    grad_den = penalty_value * grad_right

    grad_stack = planes_stack(grad_den, width)
    gy, sums = call(
        back_last_kernel, [((rows + 6, CH, LANES), f32), sums_shape],
        grad_stack, last_back_w, hidden[3], stats[3], gain_bias[3], part(inside, 3), part(own_lane, 3), name="back5",
    )
    back_stats = [None] * 4
    back_stats[3] = exchange(sums)
    own_grad = jnp.pad(
        grad_den[reach : reach + rows].reshape(rows, 2, width), ((0, 0), (0, 6), (0, LANES - width))
    ).astype(bf16)
    (grad_last,) = call(
        lambda *refs: weight_grad_kernel(*refs, rows=rows, grad_skip=0, act_skip=0, stacked=False),
        [((24, 3 * CH), f32)], own_grad, act4, name="wgrad5",
    )
    grad_middle = [None] * 3
    for layer in (3, 2, 1):
        reach = layer
        grad, gy_next, sums = call(
            lambda *refs: back_kernel(*refs, skip_in=6 - 2 * layer, skip=8 - 2 * layer),
            [((rows + 2 * reach, CH, LANES), bf16), ((rows + 2 * reach - 2, CH, LANES), f32), sums_shape],
            gy, hidden[layer], stats[layer], back_stats[layer], gain_bias[layer],
            part(valid_rows, reach), back_w[layer - 1],
            hidden[layer - 1], stats[layer - 1], gain_bias[layer - 1],
            part(inside, 7 - layer), part(own_lane, reach - 1), name=f"back{layer + 1}",
        )
        gy = gy_next
        back_stats[layer - 1] = exchange(sums)
        (grad_middle[layer - 1],) = call(
            lambda *refs: weight_grad_kernel(*refs, rows=rows, grad_skip=reach, act_skip=6 - layer, stacked=False),
            [((3 * CH, 3 * CH), f32)], grad, acts[layer - 1], name=f"wgrad{layer + 1}",
        )
    (grad_first,) = call(
        lambda *refs: first_back_kernel(*refs, hidden_skip=6, stack_skip=6),
        [((3 * CH, 8), f32)], gy, hidden[0], stats[0], back_stats[0], gain_bias[0],
        part(valid_rows, 0), stacked, name="back1",
    )

    middle = jnp.stack(grad_middle).reshape(3, 3, CH, 3 * CH)
    share = 3 * 3 * (CH // n_ch) * 3 * CH // n_img
    lane = 128 if share % 128 == 0 else share
    blocks = middle.transpose(2, 0, 1, 3).reshape(n_all * share // lane, lane)
    got = lax.all_to_all(blocks, ("ch", "img"), 0, 0, tiled=True)
    mine = jnp.sum(got.reshape(n_all, share // lane, lane), axis=0)
    mine = spread(mine, "img", n_img)
    middle_own = mine.reshape(CH // n_ch, 3, 3, 3, CH)
    grad_middle_own = middle_own.transpose(1, 3, 2, 0, 4).reshape(middle_weights.shape)

    norm_sums = jnp.stack([jnp.sum(s[::2], axis=0) for s in back_stats])
    small = jnp.concatenate(
        [grad_first.reshape(-1), grad_last.reshape(3, 8, 3 * CH)[:, :2].reshape(-1), loss_part[None], pen_part[None]]
    )
    small = jnp.pad(small, (0, rup(small.size, 1024) - small.size)).reshape(-1, 128)
    total = jnp.sum(spread(small, BOTH, n_all).reshape(n_all, -1), axis=0)
    n_first = 3 * CH * 8
    first_full = total[:n_first].reshape(3, CH, 8)[:, :, :6].reshape(3, CH, 3, 2)
    first_full = first_full.transpose(2, 0, 1, 3).reshape(9, CH, 2)
    n_last = 3 * 2 * 3 * CH
    last_full = total[n_first : n_first + n_last].reshape(3, 2, 3, CH).transpose(2, 0, 1, 3).reshape(9, 2, CH)
    loss_value = total[n_first + n_last]
    grad_penalty = total[n_first + n_last + 1]
    own = CH // n_ch
    grad_first_own = lax.dynamic_slice_in_dim(first_full, own_ch * own, own, 1)
    grad_last_own = lax.dynamic_slice_in_dim(last_full, own_ch * own, own, 2)
    norm_full = norm_sums.reshape(4, 2, CH)[:, ::-1]
    grad_norm_own = lax.dynamic_slice_in_dim(norm_full, own_ch * own, own, 2)

    step_value = step_count[0].astype(f32) + 1.0
    first_out = adamw(first_weight, grad_first_own, first_mean, first_square, rate_conv, decay_rate, step_value)
    middle_out = adamw(middle_weights, grad_middle_own, middle_mean, middle_square, rate_conv, decay_rate, step_value)
    last_out = adamw(last_weight, grad_last_own, last_mean, last_square, rate_conv, decay_rate, step_value)
    norm_out = adamw(norm_params, grad_norm_own, norm_mean, norm_square, rate_norm, 0.0, step_value)
    penalty_out = adamw(penalty, grad_penalty[None], penalty_mean, penalty_square, rate_penalty, 0.0, step_value)
    return (loss_value,) + first_out + middle_out + last_out + norm_out + (jnp.concatenate(penalty_out),)


def solution(mesh):
    in_specs = (
        P("ch", None, None, None, "img"),
        P("ch", None, None, "img", None),
        P("ch", None, "img"),
        P(None, "img", None),
        P("ch", None, "img", None),
        P(None, "ch", None),
        P(None, None, "ch", None),
        P(None, None, "ch"),
        P(None, None, "ch"),
        P(),
        P(None, "ch", None),
        P(None, "ch", None),
        P(None, None, "ch", None),
        P(None, None, "ch", None),
        P(None, None, "ch"),
        P(None, None, "ch"),
        P(None, None, "ch"),
        P(None, None, "ch"),
        P(),
        P(),
        P(),
    )
    out_specs = (
        P(),
        P(None, "ch", None),
        P(None, "ch", None),
        P(None, "ch", None),
        P(None, None, "ch", None),
        P(None, None, "ch", None),
        P(None, None, "ch", None),
        P(None, None, "ch"),
        P(None, None, "ch"),
        P(None, None, "ch"),
        P(None, None, "ch"),
        P(None, None, "ch"),
        P(None, None, "ch"),
        P(),
    )
    return jax.shard_map(body, mesh=mesh, in_specs=in_specs, out_specs=out_specs, check_vma=False)
```

```python
import math

import jax
import jax.numpy as jnp
import numpy as np
from jax import lax
from jax.experimental import pallas as pl
from jax.experimental.pallas import tpu as pltpu
from jax.sharding import PartitionSpec as P

norm_epsilon = 1e-05
beta_one = 0.9
beta_two = 0.999
adam_epsilon = 1e-08
decay_rate = 0.01
rate_conv = 0.04
rate_norm = 0.1
rate_penalty = 0.01

BOTH = ("img", "ch")
f32 = jnp.float32
bf16 = jnp.bfloat16
CH = 64
LANES = 384
HALO = 7


def rup(n, m):
    return (n + m - 1) // m * m


VM = pl.BlockSpec(memory_space=pltpu.VMEM)
SM = pl.BlockSpec(memory_space=pltpu.SMEM)
HB = pl.BlockSpec(memory_space=pltpu.HBM)


def call(kernel, ins, outs, args, scratch=(), name=None, mb=60):
    return pl.pallas_call(
        kernel,
        out_shape=[jax.ShapeDtypeStruct(shape, dtype) for shape, dtype, _ in outs],
        in_specs=ins,
        out_specs=[spec for _, _, spec in outs],
        scratch_shapes=list(scratch),
        compiler_params=pltpu.CompilerParams(vmem_limit_bytes=mb * 1024 * 1024),
        name=name,
    )(*args)


def dft_tables(n):
    k = np.arange(n)
    angle = (k[:, None] * k[None, :] % n) * (2.0 * math.pi / n)
    exact = np.concatenate([np.cos(angle), np.sin(angle)], 0) / math.sqrt(n)

    def rounded(factor):
        return (factor * exact).astype(np.float32).astype(bf16)

    def bias(factor):
        return abs(np.vdot(exact, rounded(factor).astype(np.float64) / factor) / np.vdot(exact, exact) - 1.0)

    factor = min((1.0 + 0.005 * step for step in range(201)), key=bias)
    left = lax.optimization_barrier(jnp.asarray(rounded(factor)))
    cosine, sine = left[:n], left[n:]
    right_forward = jnp.concatenate([left, jnp.concatenate([-sine, cosine], 0)], 1)
    right_back = jnp.concatenate(
        [jnp.concatenate([cosine, -sine], 0), jnp.concatenate([sine, cosine], 0)], 1
    )
    return right_forward, right_back, left, factor


def swap(values):
    return pltpu.roll(values, values.shape[-1] // 2, values.ndim - 1)


def first_half(shape):
    return lax.broadcasted_iota(jnp.int32, shape, len(shape) - 1) < shape[-1] // 2


def mm(a, b):
    return jnp.dot(a, b, preferred_element_type=f32)


def left_dft(left, values, inverse):
    rows = left.shape[0] // 2
    both = mm(left, values)
    plain, crossed = both[:rows], swap(both[rows:])
    half = first_half(plain.shape)
    crossed = jnp.where(half, crossed, -crossed)
    return plain - crossed if inverse else plain + crossed


def map_pair(cat):
    half = first_half(cat.shape)
    other = swap(cat)
    return jnp.where(half, cat, other), jnp.where(half, -other, cat)


def message_kernel(kspace, mask, maps, target, any_rows, any_cols, left, out, gathered, tall, *, at_maps):
    coils, _, cols, height = kspace.shape
    devices, length, wide = out.shape
    width = wide // 2
    rows = height // devices
    window = rows + 2 * HALO
    block = rup(window, 8)
    used = coils * cols
    half = rup(used, 128)
    pad = (tall.shape[0] - height) // 2
    gathered[...] = jnp.zeros(gathered.shape, f32)
    sampled = mask[...].astype(f32)
    for part in range(2):
        for coil in range(coils):
            at = part * half + coil * cols
            gathered[at : at + cols] = kspace[coil, part] * sampled
    tall[:pad] = jnp.zeros((pad, 2 * half), f32)
    tall[pad + height :] = jnp.zeros((pad, 2 * half), f32)
    both = outer(left[...], gathered[...].astype(bf16))
    crossed = swap(both[height:])
    crossed = jnp.where(first_half(crossed.shape), -crossed, crossed)
    tall[pad : pad + height] = both[:height] + crossed
    sampled = sampled.astype(bf16)
    per_dev = (length - at_maps) // rows - 1
    for d in range(devices):
        first = pad + d * rows - HALO
        view = tall[first : first + window].astype(bf16)
        for part in range(2):
            to = part * block
            out[d, to : to + window, :used] = view[:, part * half : part * half + used]
            out[d, to : to + cols, wide - width // 2 :] = sampled[:, part * (width // 2) : (part + 1) * (width // 2)]
        out[d, block + cols : block + cols + 2, wide - width // 2 :] = any_cols[...]
        out[d, block + cols + 2 : block + cols + 3, wide - width // 2 : wide - width // 2 + rows] = any_rows[...]
        for k in range(per_dev):
            to = at_maps + k * rows
            coil = d * per_dev + k
            if coil < coils:
                out[d, to : to + rows, :width] = maps[coil, 0].astype(bf16)
                out[d, to : to + rows, width:] = maps[coil, 1].astype(bf16)
            else:
                out[d, to : to + rows] = jnp.zeros((rows, wide), bf16)
        to = at_maps + per_dev * rows
        out[d, to : to + rows, :width] = target[0].astype(bf16)
        out[d, to : to + rows, width:] = target[1].astype(bf16)


def stack_rows(field, first, second, out):
    width = field.shape[1] // 2
    rows = out.shape[0]
    for plane_at, at in ((first, 0), (second, width)):
        plane_at[:, width:] = jnp.zeros((field.shape[0], LANES - width), f32)
        plane_at[:, :width] = field[:, at : at + width]
    out[...] = jnp.zeros(out.shape, f32)

    def move(r, carry):
        for i in range(3):
            out[r, 2 * i : 2 * i + 1, :] = first[pl.ds(r + i, 1), :]
            out[r, 2 * i + 1 : 2 * i + 2, :] = second[pl.ds(r + i, 1), :]
        return carry

    lax.fori_loop(0, rows, move, 0)


def initial_kernel(message, maps, right_back, out, stacked, spec, gathered, cat, first, second, sem, *, factor):
    copy = pltpu.make_async_copy(message.at[:, pl.ds(0, spec.shape[1])], spec, sem.at[0])
    copy.start()
    sources, length, _ = spec.shape
    block = length // 2
    coils = maps.shape[0] // 2
    rows = maps.shape[1]
    width = maps.shape[2]
    cols = width // sources
    stride = gathered.shape[0] // coils
    halo = (rows - out.shape[0]) // 2
    if stride > rows:
        gathered[...] = jnp.zeros(gathered.shape, f32)
    copy.wait()
    for s in range(sources):
        values = spec[s].astype(f32)
        for part in range(2):
            for coil in range(coils):
                to = part * width + s * cols
                gathered[coil * stride : coil * stride + rows, to : to + cols] = values[
                    part * block : part * block + rows, coil * cols : (coil + 1) * cols
                ]
    full = mm(gathered[...].astype(bf16), right_back[...])
    total = jnp.zeros((rows, 2 * width), f32)
    for coil in range(coils):
        cat[:, :width] = maps[2 * coil].astype(f32)
        cat[:, width:] = maps[2 * coil + 1].astype(f32)
        real, imag = map_pair(cat[...])
        values = full[coil * stride : coil * stride + rows]
        total = total + real * values - imag * swap(values)
    total = total * (1.0 / factor**2)
    cat[...] = total
    out[...] = cat[halo : halo + out.shape[0]]
    stack_rows(total, first, second, stacked)


class Fetch:
    def __init__(self, far, near, sems):
        self.copies = [pltpu.make_async_copy(f, n, sems.at[k]) for k, (f, n) in enumerate(zip(far, near))]
        self.near = near
        self.got = [False] * len(near)
        for copy in self.copies:
            copy.start()

    def __getitem__(self, k):
        if not self.got[k]:
            self.copies[k].wait()
            self.got[k] = True
        return self.near[k]


def apply_coils(vector, maps, mask2, right_forward, right_back, left, factor):
    total = jnp.zeros(vector.shape, f32)
    other = swap(vector)
    for coil, cat in enumerate(maps):
        real, imag = map_pair(cat()[...].astype(f32))
        sent = (real * vector + imag * other).astype(bf16)
        step = mm(sent, right_forward()[...]).astype(bf16)
        step = left_dft(left()[...], step, False) * mask2()[...].astype(f32)
        step = left_dft(left()[...], step.astype(bf16), True).astype(bf16)
        step = mm(step, right_back()[...])
        total = total + real * step - imag * swap(step)
    return total * (1.0 / factor**4)


def dot_all(a, b):
    return jnp.sum(a * b)


def operator_of(fetch, at, coils, factor):
    tables = [lambda k=k: fetch[k] for k in range(at, at + coils + 4)]
    forward, left, mask2, back = tables[0], tables[2], tables[3], tables[4]
    maps = [tables[1]] + tables[5:]
    return lambda vector: apply_coils(vector, maps, mask2, forward, back, left, factor)


def solve_first_kernel(*refs, coils, factor):
    n = coils + 5
    fetch = Fetch(refs[:n], refs[n + 1 : 2 * n + 1], refs[2 * n + 1])
    out = refs[n]
    out[...] = operator_of(fetch, 1, coils, factor)(fetch[0][...].astype(f32)).astype(bf16)


def first_step(right, applied, penalty):
    b = right.astype(f32)
    q0 = applied.astype(f32) + penalty * b
    rr0 = dot_all(b, b)
    pq0 = dot_all(b, q0)
    alpha0 = rr0 / pq0
    r1 = b - alpha0 * q0
    rn0 = dot_all(r1, r1)
    ratio0 = rn0 / rr0
    p1 = r1 + ratio0 * b
    return b, q0, rr0, pq0, alpha0, r1, rn0, ratio0, p1


def solve_second_kernel(penalty, *refs, coils, factor):
    n = coils + 6
    fetch = Fetch(refs[:n], refs[n + 1 : 2 * n + 1], refs[2 * n + 1])
    out = refs[n]
    p1 = first_step(fetch[0][...], fetch[1][...], penalty[0])[-1]
    out[...] = operator_of(fetch, 2, coils, factor)(p1).astype(bf16)


def solve_back_kernel(penalty, count, own, valid_rows, valid_cols, *refs, coils, factor):
    n = coils + 8
    fetch = Fetch(refs[:n], refs[n + 2 : 2 * n + 2], refs[2 * n + 2])
    out, scalars = refs[n : n + 2]
    tall = refs[2 * n + 3]
    lam = penalty[0]
    b, q0, rr0, pq0, alpha0, r1, rn0, ratio0, p1 = first_step(fetch[0][...], fetch[1][...], lam)
    q1 = fetch[2][...].astype(f32) + lam * p1
    pq1 = dot_all(p1, q1)
    alpha1 = rn0 / pq1
    x = alpha0 * b + alpha1 * p1
    difference = valid_rows[...] * valid_cols[...] * (x - fetch[3][...].astype(f32))
    loss = dot_all(difference, difference) / count[0]
    gx = difference * (2.0 / count[0])
    ga1 = dot_all(gx, p1)
    gpq1 = -ga1 * alpha1 / pq1
    gp = alpha1 * gx + (2.0 * gpq1) * q1
    pen = gpq1 * dot_all(p1, p1)
    grr1 = ga1 / pq1
    d1 = dot_all(gp, b)
    d2 = dot_all(gx, b)
    d4 = dot_all(gp, q0)
    d5 = dot_all(r1, q0)
    grn = grr1 + d1 / rr0
    ga = d2 - d4 - 2.0 * grn * d5
    gr = gp + (2.0 * grn) * r1
    gpq = -ga * alpha0 / pq0
    gq = gpq * b - alpha0 * gr
    grr = ga / pq0 - d1 * rn0 / (rr0 * rr0)
    pen = pen + dot_all(gq, b)
    rest = gr + ratio0 * gp + alpha0 * gx + gpq * q0 + (2.0 * grr) * b + lam * gq
    devices, window, wide = out.shape
    height = rest.shape[0]
    rows = height // devices
    pad = (tall.shape[1] - height) // 2
    for k, values in enumerate((rest, operator_of(fetch, 4, coils, factor)(gq))):
        tall[k, :pad] = jnp.zeros((pad, wide), f32)
        tall[k, pad + height :] = jnp.zeros((pad, wide), f32)
        tall[k, pad : pad + height] = values
    for d in range(devices):
        first = pad + d * rows - (window - rows) // 2
        mine = jnp.where(own[0] == d, 1.0, 0.0)
        out[d] = (tall[1, first : first + window] + mine * tall[0, first : first + window]).astype(bf16)
    lane = lax.broadcasted_iota(jnp.int32, scalars.shape, 1)
    scalars[...] = jnp.where(lane == 0, loss, jnp.where(lane == 1, pen, 0.0))


def grad_denoised_kernel(windows, denoised, penalty, stacked, scalars, cat, first, second):
    total = jnp.sum(windows[...].astype(f32), axis=0)
    cat[...] = total
    reach = (cat.shape[0] - denoised.shape[0]) // 2
    pen = dot_all(cat[reach : reach + denoised.shape[0]], denoised[...])
    scalars[...] = jnp.full(scalars.shape, pen, f32)
    stack_rows(penalty[0] * total, first, second, stacked)


def per_channel(row):
    turned = jnp.transpose(jnp.broadcast_to(row, (128, 128)))
    tiled = jnp.concatenate([turned] * (LANES // 128), axis=1)
    return tiled[:CH], tiled[CH:]


def gathered_sums(stats):
    values = stats[...]
    row = lax.broadcasted_iota(jnp.int32, values.shape, 0) % 2
    sums = jnp.sum(jnp.where(row == 0, values, 0.0), axis=0, keepdims=True)
    counts = jnp.sum(jnp.where(row == 1, values, 0.0), axis=0, keepdims=True)
    return sums, counts[:, :1]


def norm_terms(stats, gain_bias, layer):
    sums, count = gathered_sums(stats)
    means = sums / count
    average, second = per_channel(means)
    rstd = lax.rsqrt(second - average * average + norm_epsilon)
    gain, bias = per_channel(gain_bias[layer])
    return average, rstd, gain, bias


def fold(values):
    return sum(values[:, 128 * t : 128 * (t + 1)] for t in range(LANES // 128))


def write_sums(out, acc1, acc2, extra):
    both = jnp.concatenate([acc1, acc2], axis=0)
    row = jnp.sum(jnp.transpose(both), axis=0, keepdims=True)
    second = jnp.broadcast_to(extra, row.shape)
    which = lax.broadcasted_iota(jnp.int32, out.shape, 0) % 2
    out[...] = jnp.where(which == 0, row, second)


def plan(count):
    for rows in (10, 12, 11, 13, 14, 9, 8):
        if count % rows == 0:
            return rows, count // rows, 0
    if count <= 14:
        return count, 1, 0
    return 10, count // 10, count % 10


class Rows:
    def __init__(self, hbm, vmem, sems, count, base=0, lead=0, inward=True):
        self.hbm, self.vmem, self.sems = hbm, vmem, sems
        self.count, self.base, self.lead, self.inward = count, base, lead, inward
        self.rows, self.whole, self.rest = plan(count)

    def copy(self, at, rows, slot):
        far = self.hbm.at[pl.ds(at + self.base, rows)]
        near = self.vmem.at[pl.ds(at, rows)]
        if self.inward:
            return pltpu.make_async_copy(far, near, self.sems.at[slot])
        return pltpu.make_async_copy(near, far, self.sems.at[slot])

    def block(self, t, rows):
        return self.copy(t * self.rows + self.lead, rows, t)

    def head(self):
        return self.copy(0, self.lead, self.whole + 1)

    def each(self, action):
        def one(t, carry):
            action(self.block(t, self.rows))
            return carry

        lax.fori_loop(0, self.whole, one, 0)
        if self.rest:
            action(self.block(self.whole, self.rest))

    def start(self):
        if self.lead:
            self.head().start()
        self.each(lambda copy: copy.start())

    def wait(self):
        self.each(lambda copy: copy.wait())


def over_rows(count, step, carry):
    rows, whole, rest = plan(count)
    carry = lax.fori_loop(0, whole, lambda t, state: step(t, t * rows, rows, state), carry)
    if rest:
        carry = step(whole, whole * rows, rest, carry)
    return carry


def sems(count):
    return pltpu.SemaphoreType.DMA((plan(count)[1] + 2,))


def plane(dtype, rows):
    return pltpu.VMEM((rows, CH, LANES), dtype)


def zero_sums():
    return jnp.zeros((CH, 128), f32), jnp.zeros((CH, 128), f32)


def beside(values):
    return values[0] if len(values) == 1 else jnp.concatenate(values, axis=1)


def lanes_of(values, u):
    return values[:, u * LANES : (u + 1) * LANES]


def taps_sum(y):
    n = y.shape[0] // 3
    return pltpu.roll(y[:n], 1, 1) + y[n : 2 * n] + pltpu.roll(y[2 * n :], LANES - 1, 1)


def taps(rows8):
    return jnp.concatenate([pltpu.roll(rows8, 1, 1), rows8, pltpu.roll(rows8, LANES - 1, 1)], axis=0).astype(bf16)


def first_conv_kernel(stacked, weight, mask, count, out_hbm, sums, out, out_sems):
    n = out.shape[0]
    at = (mask.shape[0] - n) // 2
    store = Rows(out_hbm, out, out_sems, n, inward=False)
    w = weight[...]

    def step(t, r0, rows, acc):
        y = mm(w, beside([taps(stacked[r0 + u]) for u in range(rows)]))
        for u in range(rows):
            value = lanes_of(y, u)
            out[r0 + u] = value.astype(bf16)
            kept = value * mask[pl.ds(r0 + u + at, 1), :]
            acc = acc[0] + fold(kept), acc[1] + fold(kept * value)
        store.block(t, rows).start()
        return acc

    acc = over_rows(n, step, zero_sums())
    write_sums(sums, *acc, count[0])
    store.wait()


def activation(hidden, stats, gain_bias, layer, inside, at):
    average, rstd, gain, bias = norm_terms(stats, gain_bias, layer)
    scale = gain * rstd
    shift = bias - average * scale

    def activate(r):
        return (jnp.maximum(hidden[r].astype(f32) * scale + shift, 0.0) * inside[pl.ds(r + at, 1), :]).astype(bf16)

    return activate


def three_rows(values):
    return beside([jnp.concatenate(values[u : u + 3], axis=0) for u in range(len(values) - 2)])


def conv_kernel(
    hidden_hbm, stats, gain_bias, weight, inside, mask, count, out_hbm, sums, hidden, out, in_sems, out_sems, *, layer
):
    n = out.shape[0]
    at = (mask.shape[0] - n) // 2
    load = Rows(hidden_hbm, hidden, in_sems, n, lead=2)
    store = Rows(out_hbm, out, out_sems, n, inward=False)
    load.start()
    activate = activation(hidden, stats, gain_bias, layer, inside, at - 1)
    w = weight[layer]
    load.head().wait()

    def step(t, r0, rows, acc):
        load.block(t, rows).wait()
        y = mm(w, three_rows([activate(r0 + u) for u in range(rows + 2)]))
        for u in range(rows):
            value = taps_sum(lanes_of(y, u))
            out[r0 + u] = value.astype(bf16)
            kept = value * mask[pl.ds(r0 + u + at, 1), :]
            acc = acc[0] + fold(kept), acc[1] + fold(kept * value)
        store.block(t, rows).start()
        return acc

    acc = over_rows(n, step, zero_sums())
    write_sums(sums, *acc, count[0])
    store.wait()


def last_conv_kernel(
    hidden_hbm, stats, gain_bias, weight, inside, initial, penalty, denoised, right, hidden, branch, in_sems, *, base
):
    n, wide = branch.shape
    width = wide // 2
    load = Rows(hidden_hbm, hidden, in_sems, n, base=base, lead=2)
    load.start()
    activate = activation(hidden, stats, gain_bias, 3, inside, HALO - 1)
    w = weight[...]
    load.head().wait()

    def step(t, r0, rows, carry):
        load.block(t, rows).wait()
        y = mm(w, three_rows([activate(r0 + u) for u in range(rows + 2)]))
        for u in range(rows):
            value = taps_sum(lanes_of(y, u))
            branch[pl.ds(r0 + u, 1), :width] = value[0:1, :width]
            branch[pl.ds(r0 + u, 1), width:] = value[1:2, :width]
        return carry

    over_rows(n, step, 0)
    sent = initial[...]
    result = sent + branch[...]
    denoised[...] = result
    sent = (sent + penalty[0] * result).astype(bf16)
    for d in range(right.shape[0]):
        right[d] = sent


def moments_kernel(hidden_hbm, stats, gain_bias, mask, stacked, out, hidden, in_sems, *, base, stack_base):
    n = hidden.shape[0]
    load = Rows(hidden_hbm, hidden, in_sems, n, base=base)
    load.start()
    average, rstd, _, _ = norm_terms(stats, gain_bias, 0)
    out[...] = jnp.zeros(out.shape, f32)

    def step(t, r0, rows, carry):
        load.block(t, rows).wait()
        left = []
        for u in range(rows):
            valid = jnp.broadcast_to(mask[pl.ds(r0 + u + HALO, 1), :], (8, LANES))
            normed = (hidden[r0 + u].astype(f32) - average) * rstd * mask[pl.ds(r0 + u + HALO, 1), :]
            left.append(jnp.concatenate([normed, valid], axis=0).astype(bf16))
        out[...] += outer(beside(left), beside([taps(stacked[r0 + stack_base + u]) for u in range(rows)]))
        return carry

    over_rows(n, step, 0)


def grad_tail(ga, hidden_row, terms, inside_row):
    average, rstd, gain, bias = terms
    normed = (hidden_row.astype(f32) - average) * rstd
    keep = (gain * normed + bias > 0.0) & (inside_row > 0.0)
    return jnp.where(keep, ga, 0.0), normed


def back_last_kernel(
    stacked, weight, hidden_hbm, stats, gain_bias, inside, own, gy_hbm, sums, hidden, gy, in_sems, out_sems
):
    n = gy.shape[0]
    at = (inside.shape[0] - n) // 2
    load = Rows(hidden_hbm, hidden, in_sems, n)
    store = Rows(gy_hbm, gy, out_sems, n, inward=False)
    load.start()
    terms = norm_terms(stats, gain_bias, 3)
    w = weight[...]

    def step(t, r0, rows, acc):
        load.block(t, rows).wait()
        y = mm(w, beside([taps(stacked[r0 + u]) for u in range(rows)]))
        for u in range(rows):
            value, normed = grad_tail(lanes_of(y, u), hidden[r0 + u], terms, inside[pl.ds(r0 + u + at, 1), :])
            gy[r0 + u] = value.astype(bf16)
            kept = value * own[pl.ds(r0 + u + at, 1), :]
            acc = acc[0] + fold(kept), acc[1] + fold(kept * normed)
        store.block(t, rows).start()
        return acc

    acc = over_rows(n, step, zero_sums())
    write_sums(sums, *acc, 0.0)
    store.wait()


def hidden_grad_terms(stats, back_stats, gain_bias, layer):
    average, rstd, gain, _ = norm_terms(stats, gain_bias, layer)
    _, count = gathered_sums(stats)
    back, _ = gathered_sums(back_stats)
    s1, s2 = per_channel(back / count)
    return average, rstd, gain * rstd, s1, s2


def back_kernel(
    gy_in_hbm, hidden_in_hbm, stats_in, back_stats, gain_bias, mask,
    weight, hidden_hbm, stats, inside, own, *rest, layer
):
    final = layer == 1
    skip_in, skip = 6 - 2 * layer, 8 - 2 * layer
    if final:
        stacked, cross, grad_hbm, sums = rest[0], rest[1], rest[2], rest[3]
        gy_in, hidden_in, hidden, grad, s_gy, s_hin, s_hid, s_grad = rest[4:]
        stack_base = (stacked.shape[0] - hidden.shape[0]) // 2
    else:
        grad_hbm, gy_hbm, sums = rest[0], rest[1], rest[2]
        gy_in, hidden_in, hidden, grad, gy, s_gy, s_hin, s_hid, s_grad, s_out = rest[3:]
    n = hidden.shape[0]
    at = (inside.shape[0] - n) // 2
    load_gy = Rows(gy_in_hbm, gy_in, s_gy, n, lead=2)
    load_in = Rows(hidden_in_hbm, hidden_in, s_hin, n, base=skip_in, lead=2)
    load = Rows(hidden_hbm, hidden, s_hid, n, base=skip)
    store_grad = Rows(grad_hbm, grad, s_grad, n, lead=2, inward=False)
    for group in (load_gy, load_in, load):
        group.start()
    average, rstd, scale, s1, s2 = hidden_grad_terms(stats_in, back_stats, gain_bias, layer)
    terms = norm_terms(stats, gain_bias, layer - 1)
    w = weight[layer - 1]

    def hidden_grad(r):
        normed = (hidden_in[r].astype(f32) - average) * rstd
        return (scale * (gy_in[r].astype(f32) - mask[pl.ds(r + at - 1, 1), :] * (s1 + normed * s2))).astype(bf16)

    load_gy.head().wait()
    load_in.head().wait()
    for r in range(2):
        grad[r] = hidden_grad(r)
    store_grad.head().start()
    if final:
        cross[...] = jnp.zeros(cross.shape, f32)
    else:
        store = Rows(gy_hbm, gy, s_out, n, inward=False)

    def step(t, r0, rows, acc):
        load_gy.block(t, rows).wait()
        load_in.block(t, rows).wait()
        load.block(t, rows).wait()
        grads = [hidden_grad(r0 + u) for u in range(rows + 2)]
        for u in range(2, rows + 2):
            grad[r0 + u] = grads[u]
        store_grad.block(t, rows).start()
        y = mm(w, three_rows(grads))
        values = []
        for u in range(rows):
            value, normed = grad_tail(taps_sum(lanes_of(y, u)), hidden[r0 + u], terms, inside[pl.ds(r0 + u + at, 1), :])
            kept = value * own[pl.ds(r0 + u + at, 1), :]
            acc = acc[0] + fold(kept), acc[1] + fold(kept * normed)
            if final:
                values.append(value.astype(bf16))
            else:
                gy[r0 + u] = value.astype(bf16)
        if final:
            cross[...] += outer(beside(values), beside([taps(stacked[r0 + stack_base + u]) for u in range(rows)]))
        else:
            store.block(t, rows).start()
        return acc

    acc = over_rows(n, step, zero_sums())
    write_sums(sums, *acc, 0.0)
    store_grad.head().wait()
    store_grad.wait()
    if not final:
        store.wait()


def shifted(row):
    wide = row.astype(f32)
    return jnp.concatenate(
        [pltpu.roll(wide, LANES - 1, 1).astype(bf16), row, pltpu.roll(wide, 1, 1).astype(bf16)], axis=0
    )


def outer(a, b):
    return lax.dot_general(a, b, (((1,), (1,)), ((), ())), preferred_element_type=f32)


def weight_grad_kernel(
    grad_hbm, hidden_hbm, stats, gain_bias, inside, out, grad, hidden, s_grad, s_hid, *, layer
):
    n = grad.shape[0]
    load_grad = Rows(grad_hbm, grad, s_grad, n, base=layer)
    load = Rows(hidden_hbm, hidden, s_hid, n, base=6 - layer, lead=2)
    load.start()
    load_grad.start()
    activate = activation(hidden, stats, gain_bias, layer - 1, inside, HALO - 1)
    out[...] = jnp.zeros(out.shape, f32)
    load.head().wait()

    def step(t, r0, rows, carry):
        load.block(t, rows).wait()
        load_grad.block(t, rows).wait()
        left = beside([shifted(grad[r0 + u]) for u in range(rows)])
        right = three_rows([activate(r0 + u) for u in range(rows + 2)])
        out[...] += outer(left, right)
        return carry

    over_rows(n, step, 0)


def last_weight_grad_kernel(stacked, hidden_hbm, stats, gain_bias, inside, out, hidden, in_sems, *, base, stack_base):
    n = hidden.shape[0]
    load = Rows(hidden_hbm, hidden, in_sems, n, base=base)
    load.start()
    activate = activation(hidden, stats, gain_bias, 3, inside, HALO)
    out[...] = jnp.zeros(out.shape, f32)

    def step(t, r0, rows, carry):
        load.block(t, rows).wait()
        left = beside([activate(r0 + u) for u in range(rows)])
        out[...] += outer(left, beside([taps(stacked[r0 + stack_base + u]) for u in range(rows)]))
        return carry

    over_rows(n, step, 0)


def spread(values, axes, size):
    wide = jnp.broadcast_to(values[None], (size,) + values.shape).reshape((size * values.shape[0],) + values.shape[1:])
    return lax.all_to_all(wide, axes, 0, 0, tiled=True)


def row_shift(values, hops):
    size = lax.axis_size("img")
    pairs = [(i, i + hops) for i in range(size) if 0 <= i + hops < size]
    return lax.ppermute(values, "img", pairs)


def with_halo(values, width):
    rows = values.shape[1]
    before, after = [], []
    need, hop = width, 1
    while need > 0:
        part = min(need, rows)
        before.insert(0, row_shift(values[:, rows - part :], hop))
        after.append(row_shift(values[:, :part], -hop))
        need -= part
        hop += 1
    return jnp.concatenate(before + [values] + after, axis=1)


def tap_weights(values):
    values = values.reshape(CH, 3, 3, 2).transpose(0, 2, 1, 3).reshape(CH, 3, 6)
    return jnp.pad(values, ((0, 0), (0, 0), (0, 2))).reshape(CH, 24)


def adamw(weight, grad, first_m, second_m, rate, decay, step_value):
    mean_new = beta_one * first_m + (1.0 - beta_one) * grad
    square_new = beta_two * second_m + (1.0 - beta_two) * grad * grad
    mean_hat = mean_new / (1.0 - beta_one**step_value)
    square_hat = square_new / (1.0 - beta_two**step_value)
    updated = weight - rate * (mean_hat / (jnp.sqrt(square_hat) + adam_epsilon) + decay * weight)
    return (updated, mean_new, square_new)


def body(
    kspace_data, coil_maps, sample_mask, valid_mask, target,
    first_weight, middle_weights, last_weight, norm_params, penalty,
    first_mean, first_square, middle_mean, middle_square, last_mean, last_square,
    norm_mean, norm_square, penalty_mean, penalty_square, step_count,
):
    n_img = lax.axis_size("img")
    n_ch = lax.axis_size("ch")
    n_all = n_img * n_ch
    own_ch = lax.axis_index("ch")
    own_img = lax.axis_index("img")
    coils = kspace_data.shape[1]
    height = kspace_data.shape[3]
    width = coil_maps.shape[4]
    rows = coil_maps.shape[3]
    cols = kspace_data.shape[4]
    wide = 2 * width
    per_dev = -(-coils // n_img)
    right_forward, right_back, left, factor = dft_tables(width)

    window = rows + 2 * HALO
    block = rup(window, 8)
    half = rup(coils * cols, 128)
    at_maps = 2 * block
    length = at_maps + (per_dev + 1) * rows
    valid_own = lax.dynamic_index_in_dim(valid_mask, own_ch, 0, keepdims=False).astype(f32)
    any_rows = jnp.max(valid_own, 1).astype(bf16)[None]
    any_cols = jnp.max(valid_own, 0).astype(bf16).reshape(2, width // 2)
    (message,) = call(
        lambda *refs: message_kernel(*refs, at_maps=at_maps), [VM] * 7, [((n_img, length, wide), bf16, VM)],
        (kspace_data[0].transpose(0, 1, 3, 2), sample_mask[0].T, coil_maps[0], target[0], any_rows, any_cols, left),
        scratch=[pltpu.VMEM((2 * half, height), f32), pltpu.VMEM((height + 16, 2 * half), f32)], name="message",
    )

    packed = jnp.concatenate(
        [middle_weights.reshape(-1), first_weight.reshape(-1), last_weight.reshape(-1), norm_params.reshape(-1)]
    )
    packed = jnp.pad(packed, (0, rup(packed.size, 1024) - packed.size)).reshape(-1, 128)
    planes = coil_maps[0].reshape(2 * coils, rows, width).astype(bf16)
    message, packed, planes = lax.optimization_barrier((message, packed, planes))
    message = lax.all_to_all(message, "img", 0, 0, tiled=True)
    everyone = jnp.zeros((n_ch,) + packed.shape, f32)
    for hop in range(n_ch):
        came = packed if hop == 0 else lax.ppermute(packed, "ch", [(i, (i + hop) % n_ch) for i in range(n_ch)])
        everyone = lax.dynamic_update_index_in_dim(everyone, came, (own_ch - hop) % n_ch, 0)
    tall_maps = with_halo(planes, HALO)
    initial, stacked = call(
        lambda *refs: initial_kernel(*refs, factor=factor), [HB, VM, VM],
        [((rows, wide), f32, VM), ((window - 2, 8, LANES), f32, VM)],
        (message, tall_maps, right_back),
        scratch=[
            pltpu.VMEM((n_img, at_maps, wide), bf16), pltpu.VMEM((coils * rup(window, 8), wide), f32),
            pltpu.VMEM((window, wide), f32), pltpu.VMEM((window, LANES), f32), pltpu.VMEM((window, LANES), f32),
            pltpu.SemaphoreType.DMA((1,)),
        ],
        name="initial",
    )

    sizes = [middle_weights.size, first_weight.size, last_weight.size, norm_params.size]
    cuts = np.cumsum([0] + sizes)
    shapes = [middle_weights.shape, first_weight.shape, last_weight.shape, norm_params.shape]
    channel_dim = [2, 1, 2, 2]

    def full(k):
        piece = everyone.reshape(n_ch, -1)[:, cuts[k] : cuts[k + 1]].reshape((n_ch,) + shapes[k])
        piece = jnp.moveaxis(piece, 0, channel_dim[k])
        dims = list(shapes[k])
        dims[channel_dim[k]] *= n_ch
        return piece.reshape(dims)

    middle_all, first_all, last_all, norms_all = (full(k) for k in range(4))
    low = middle_all.astype(bf16).reshape(3, 3, 3, CH, CH)
    forward_w = low.transpose(0, 2, 3, 1, 4).reshape(3, 3 * CH, 3 * CH)
    back_w = low[:, ::-1, ::-1].transpose(0, 2, 4, 1, 3).reshape(3, 3 * CH, 3 * CH)
    first_w = tap_weights(first_all.astype(bf16).transpose(1, 0, 2))
    last_low = last_all.astype(bf16)
    last_w = last_low.reshape(3, 3, 2, CH).transpose(1, 2, 0, 3)
    last_w = jnp.pad(last_w, ((0, 0), (0, 6), (0, 0), (0, 0))).reshape(24, 3 * CH)
    last_back_w = tap_weights(last_low[::-1].transpose(2, 0, 1))
    gain_bias = norms_all.reshape(4, 1, 2 * CH)

    row_at = own_img * rows - HALO + jnp.arange(rows + 2 * HALO)
    in_image = ((row_at >= 0) & (row_at < height)).astype(f32)
    in_lane = (jnp.arange(LANES) < width).astype(f32)
    inside = in_image[:, None] * in_lane[None, :]
    is_own = ((row_at >= own_img * rows) & (row_at < (own_img + 1) * rows)).astype(f32)
    own_valid = jnp.pad(valid_own, ((HALO, HALO), (0, LANES - width)))
    own_lane = is_own[:, None] * in_lane[None, :]
    local_count = jnp.sum(valid_own)[None]

    def exchange(values):
        return lax.all_to_all(values, BOTH, 0, 0, tiled=True)

    sums_out = ((2 * n_all, 128), f32, VM)

    def hidden_out(reach):
        return ((rows + 2 * reach, CH, LANES), bf16, HB)

    out, sums = call(
        first_conv_kernel, [VM, VM, VM, SM], [hidden_out(6), sums_out],
        (stacked, first_w, own_valid, local_count),
        scratch=[plane(bf16, rows + 12), sems(rows + 12)], name="conv1",
    )
    hidden = [out]
    stats = [exchange(sums)]
    for layer in range(3):
        n = rows + 10 - 2 * layer
        out, sums = call(
            lambda *refs: conv_kernel(*refs, layer=layer), [HB] + [VM] * 5 + [SM], [hidden_out(5 - layer), sums_out],
            (hidden[layer], stats[layer], gain_bias, forward_w, inside, own_valid, local_count),
            scratch=[plane(bf16, n + 2), plane(bf16, n), sems(n), sems(n)], name=f"conv{layer + 2}",
        )
        hidden.append(out)
        stats.append(exchange(sums))
    denoised, right = call(
        lambda *refs: last_conv_kernel(*refs, base=2), [HB] + [VM] * 5 + [SM],
        [((rows, wide), f32, VM), ((n_img, rows, wide), bf16, VM)],
        (hidden[3], stats[3], gain_bias, last_w, inside, initial, penalty),
        scratch=[plane(bf16, rows + 2), pltpu.VMEM((rows, wide), f32), sems(rows)], name="conv5",
    )

    pieces = [
        message[:, at_maps + c * rows : at_maps + (c + 1) * rows].reshape(height, wide) for c in range(per_dev + 1)
    ]
    maps_full, target_full = pieces[:per_dev], pieces[per_dev]
    flags = message[:, : 2 * block, wide - width // 2 :].reshape(n_img, 2, block, width // 2)
    turned = jnp.concatenate([flags[:, p, :cols].reshape(width, width // 2).T for p in range(2)], axis=0)
    mask2 = jnp.concatenate([turned, turned], axis=1)
    rest = flags[:, 1, cols:].astype(f32)
    valid_cols = jnp.max(rest[:, :2], axis=0).reshape(width)
    valid_rows = rest[:, 2, :rows].reshape(height)
    near_rows = lax.dynamic_slice_in_dim(jnp.pad(valid_rows, (HALO, HALO)), own_img * rows, rows + 2 * HALO, 0)
    valid_near = near_rows[:, None] * jnp.pad(valid_cols, (0, LANES - width))[None, :]
    valid_rows = valid_rows[:, None]
    valid_cols = jnp.concatenate([valid_cols, valid_cols])[None, :]
    operator_args = [right_forward, maps_full[0], left, mask2, right_back] + maps_full[1:]

    def send(values):
        return lax.all_to_all(values, "img", 0, 0, tiled=True)

    def solve(kernel, scalars, vmem, arrays, outs, name, extra=()):
        arrays = list(arrays) + operator_args
        return call(
            lambda *refs: kernel(*refs, coils=per_dev, factor=factor), [SM] * len(scalars) + [VM] * len(vmem) + [HB] * len(arrays), outs,
            (*scalars, *vmem, *arrays),
            scratch=[pltpu.VMEM(a.shape, a.dtype) for a in arrays] + [pltpu.SemaphoreType.DMA((len(arrays),))] + list(extra),
            name=name,
        )

    def gathered(partial):
        got = send(partial.reshape(n_img, rows, wide))
        total = jnp.sum(got.astype(f32), axis=0).astype(bf16)
        return send(jnp.broadcast_to(total[None], (n_img, rows, wide))).reshape(height, wide)

    whole = ((height, wide), bf16, VM)
    right = send(right).reshape(height, wide)
    (partial,) = solve(solve_first_kernel, (), (), (right,), [whole], "solve1")
    applied0 = gathered(partial)
    (partial,) = solve(solve_second_kernel, (penalty,), (), (right, applied0), [whole], "solve2")
    applied1 = gathered(partial)
    count = jnp.sum(stats[0][1::2, 0])[None]
    (moments,) = call(
        lambda *refs: moments_kernel(*refs, base=6, stack_base=6), [HB] + [VM] * 4, [((CH + 8, 24), f32, VM)],
        (hidden[0], stats[0], gain_bias, own_valid, stacked),
        scratch=[plane(bf16, rows), sems(rows)], name="moments",
    )
    tall_rows = rows + 8
    windows, scalars = solve(
        solve_back_kernel, (penalty, count, own_img.astype(jnp.int32)[None]), (valid_rows, valid_cols),
        (right, applied0, applied1, target_full),
        [((n_img, tall_rows, wide), bf16, VM), ((8, 128), f32, VM)], "solve3",
        extra=[pltpu.VMEM((2, height + 16, wide), f32)],
    )
    windows = send(windows)
    windows, moments = lax.optimization_barrier((windows, moments))
    grad_stack, pen_own = call(
        grad_denoised_kernel, [VM, VM, SM], [((rows + 6, 8, LANES), f32, VM), ((8, 128), f32, VM)],
        (windows, denoised, penalty),
        scratch=[
            pltpu.VMEM((tall_rows, wide), f32), pltpu.VMEM((tall_rows, LANES), f32), pltpu.VMEM((tall_rows, LANES), f32),
        ],
        name="grad_denoised",
    )
    pen_part = scalars[0, 1] / n_img + pen_own[0, 0]
    loss_part = scalars[0, 0] / n_img

    n = rows + 6
    gy, sums = call(
        back_last_kernel, [VM, VM, HB] + [VM] * 4, [hidden_out(3), sums_out],
        (grad_stack, last_back_w, hidden[3], stats[3], gain_bias, inside, own_lane),
        scratch=[plane(bf16, n), plane(bf16, n), sems(n), sems(n)], name="back5",
    )
    back_stats = [None] * 4
    back_stats[3] = exchange(sums)
    (grad_last,) = call(
        lambda *refs: last_weight_grad_kernel(*refs, base=3, stack_base=3),
        [VM, HB] + [VM] * 3, [((CH, 24), f32, VM)],
        (grad_stack, hidden[3], stats[3], gain_bias, inside),
        scratch=[plane(bf16, rows), sems(rows)], name="wgrad5",
    )
    back_stats[3], grad_last = lax.optimization_barrier((back_stats[3], grad_last))
    grad_middle = [None] * 3
    cross = None
    for layer in (3, 2, 1):
        n = rows + 2 * layer - 2
        final = layer == 1
        ins = [HB, HB] + [VM] * 5 + [HB] + [VM] * 3
        args = (
            gy, hidden[layer], stats[layer], back_stats[layer], gain_bias, valid_near,
            back_w, hidden[layer - 1], stats[layer - 1], inside, own_lane,
        )
        scratch = [plane(bf16, n + 2), plane(bf16, n + 2), plane(bf16, n), plane(bf16, n + 2)]
        kernel = lambda *refs: back_kernel(*refs, layer=layer)
        if final:
            cross, grad, sums = call(
                kernel, ins + [VM], [((CH, 24), f32, VM), hidden_out(layer), sums_out], args + (stacked,),
                scratch=scratch + [sems(n)] * 4, name="back2",
            )
        else:
            grad, gy, sums = call(
                kernel, ins, [hidden_out(layer), hidden_out(layer - 1), sums_out], args,
                scratch=scratch + [plane(bf16, n)] + [sems(n)] * 5, name=f"back{layer + 1}",
            )
            back_stats[layer - 1] = exchange(sums)
        (grad_middle[layer - 1],) = call(
            lambda *refs: weight_grad_kernel(*refs, layer=layer),
            [HB, HB] + [VM] * 3, [((3 * CH, 3 * CH), f32, VM)],
            (grad, hidden[layer - 1], stats[layer - 1], gain_bias, inside),
            scratch=[plane(bf16, rows), plane(bf16, rows + 2), sems(rows), sems(rows)], name=f"wgrad{layer + 1}",
        )
        if not final:
            back_stats[layer - 1], grad_middle[layer - 1] = lax.optimization_barrier(
                (back_stats[layer - 1], grad_middle[layer - 1])
            )

    own = CH // n_ch
    sums_row = sums[0]
    small = jnp.concatenate(
        [
            cross, grad_last, moments[:CH], sums_row[:CH, None], sums_row[CH:, None],
            jnp.full((CH, 1), loss_part), jnp.full((CH, 1), pen_part), jnp.zeros((CH, 4), f32),
            jnp.broadcast_to(moments[CH : CH + 1], (CH, 24)), jnp.zeros((CH, 24), f32),
        ],
        axis=1,
    )
    small = jnp.broadcast_to(small.reshape(1, n_ch, own, 128), (n_img, n_ch, own, 128)).reshape(n_all, own, 128)
    share = 27 * own * CH // n_img
    lane = 128 if share % 128 == 0 else share
    middle = jnp.stack(grad_middle).reshape(3, 3, n_ch, n_img, own * CH * 3 // n_img)
    if own % n_img == 0:
        blocks = middle.transpose(3, 2, 0, 1, 4)
    else:
        blocks = jnp.stack(grad_middle).reshape(9, n_ch, own * 3 * CH).transpose(1, 0, 2)
        blocks = blocks.reshape(n_ch, n_img, share).transpose(1, 0, 2)
    blocks = blocks.reshape(n_all, share // lane, lane)
    if lane == 128:
        got = exchange(jnp.concatenate([small, blocks], axis=1))
        total = jnp.sum(got.reshape(n_all, own + share // 128, 128), axis=0)
        small_total, mine = total[:own], total[own:]
    else:
        small_total = jnp.sum(exchange(small), axis=0)
        mine = jnp.sum(exchange(blocks), axis=0)
    mine = spread(mine, "img", n_img)
    if own % n_img == 0:
        middle_own = mine.reshape(n_img, 3, 3, own // n_img, 3, CH)
        grad_middle_own = middle_own.transpose(1, 4, 2, 0, 3, 5).reshape(middle_weights.shape)
    else:
        middle_own = mine.reshape(3, 3, own, 3, CH)
        grad_middle_own = middle_own.transpose(0, 3, 1, 2, 4).reshape(middle_weights.shape)

    means, pixels = gathered_sums_plain(stats[0])
    norms_own = lax.dynamic_slice_in_dim(norms_all, own_ch * own, own, 2)
    average = lax.dynamic_slice_in_dim(means[:CH] / pixels, own_ch * own, own, 0)
    second = lax.dynamic_slice_in_dim(means[CH:] / pixels, own_ch * own, own, 0)
    scale = norms_own[0, 0] * lax.rsqrt(second - average * average + norm_epsilon)
    s1, s2 = small_total[:, 72:73], small_total[:, 73:74]
    first_total = scale[:, None] * (
        small_total[:, :24] - (s1 * small_total[:, 80:104] + s2 * small_total[:, 48:72]) / pixels
    )

    def tap_major(values):
        return values.reshape(own, 3, 8)[:, :, :6].reshape(own, 3, 3, 2).transpose(2, 1, 0, 3).reshape(9, own, 2)

    grad_first_own = tap_major(first_total)
    grad_last_own = tap_major(small_total[:, 24:48])[::-1].transpose(0, 2, 1)
    loss_value = small_total[0, 74]
    grad_penalty = small_total[0, 75]
    later = jnp.stack([jnp.sum(s[::2], axis=0) for s in back_stats[1:]]).reshape(3, 2, CH)
    later = lax.dynamic_slice_in_dim(later, own_ch * own, own, 2)
    grad_norm_own = jnp.concatenate([jnp.stack([s1[:, 0], s2[:, 0]])[None], later], axis=0)[:, ::-1]

    step_value = step_count[0].astype(f32) + 1.0
    first_out = adamw(first_weight, grad_first_own, first_mean, first_square, rate_conv, decay_rate, step_value)
    middle_out = adamw(middle_weights, grad_middle_own, middle_mean, middle_square, rate_conv, decay_rate, step_value)
    last_out = adamw(last_weight, grad_last_own, last_mean, last_square, rate_conv, decay_rate, step_value)
    norm_out = adamw(norm_params, grad_norm_own, norm_mean, norm_square, rate_norm, 0.0, step_value)
    penalty_out = adamw(penalty, grad_penalty[None], penalty_mean, penalty_square, rate_penalty, 0.0, step_value)
    return (loss_value,) + first_out + middle_out + last_out + norm_out + (jnp.concatenate(penalty_out),)


def gathered_sums_plain(stats):
    return jnp.sum(stats[::2], axis=0), jnp.sum(stats[1::2, 0])


def solution(mesh):
    in_specs = (
        P("ch", None, None, None, "img"),
        P("ch", None, None, "img", None),
        P("ch", None, "img"),
        P(None, "img", None),
        P("ch", None, "img", None),
        P(None, "ch", None),
        P(None, None, "ch", None),
        P(None, None, "ch"),
        P(None, None, "ch"),
        P(),
        P(None, "ch", None),
        P(None, "ch", None),
        P(None, None, "ch", None),
        P(None, None, "ch", None),
        P(None, None, "ch"),
        P(None, None, "ch"),
        P(None, None, "ch"),
        P(None, None, "ch"),
        P(),
        P(),
        P(),
    )
    out_specs = (
        P(),
        P(None, "ch", None),
        P(None, "ch", None),
        P(None, "ch", None),
        P(None, None, "ch", None),
        P(None, None, "ch", None),
        P(None, None, "ch", None),
        P(None, None, "ch"),
        P(None, None, "ch"),
        P(None, None, "ch"),
        P(None, None, "ch"),
        P(None, None, "ch"),
        P(None, None, "ch"),
        P(),
    )
    return jax.shard_map(body, mesh=mesh, in_specs=in_specs, out_specs=out_specs, check_vma=False)
```
